256 devices in a mesh: dom: 64 (over x, z, core), head: 4 (over y).
Axes of the slice: x: 4, y: 4, z: 8, core: 2. Of those that a mesh axis runs over, the one named last changes fastest.
Arguments:
- features: bfloat16 [65536, 512], P('dom'), may hold values from -16 to 16
- norm_gain: float32 [512], replicated, may hold values from 0.25 to 1.75
- qkv_weight: bfloat16 [3, 512, 512], P(None, None, 'head'), may hold values from -0.25 to 0.25
- out_weight: bfloat16 [512, 512], P(None, 'head'), may hold values from -1 to 1
- edge_bias: float32 [8, 7, 65536], P('head', None, 'dom'), may hold values from -300 to 300
- band_mask: int32 [2, 512], P(None, 'dom'), may hold values 0 or 1
- matchings: int32 [4, 512], P(None, 'dom'), may hold values from 0 to 511, as said below
- cotangent: bfloat16 [65536, 512], P('dom'), may hold values from -16 to 16
Outputs:
- layer_out: bfloat16 [65536, 512], P('dom', 'head')
- grad_input: bfloat16 [65536, 512], P('dom', 'head')
- grad_qkv: float32 [3, 512, 512], P(None, 'dom', 'head')
- grad_out: float32 [512, 512], P('dom', 'head')
The draws below stay inside these ranges and needn't reach their ends.
Inputs may be any that keep to these rules, and one draw needn't show every extreme that they name: `band_mask`: entry [0, b] says whether block b's nodes attend to block b - 1 and entry [1, b] to block b + 1; the left flag of block 0 and the right flag of the last block are not used. Each row is a matching of the 512 blocks: matchings[j, matchings[j, b]] = b, and a block may be its own partner. Over the four rows together, the 8 blocks of one device (blocks d * 8 to (d + 1) * 8 - 1) are matched to exactly 1 block of each of min(32, 64) devices, its own included, and to no block of any other device.
All inputs are finite; a program needn't handle non-finite values.
Results may differ from the reference program's by a relative error of at most 0.014.
Values may be sent and summed in bfloat16 or wider, within the bound.
No kernel may reach another device: no remote copies, remote signals or barrier semaphores. Data moves between devices by JAX's collectives and lax.ppermute only.
A program may use at most 128 MiB of HBM per device.

```python
import math
import jax
import jax.numpy as jnp
from jax import lax

D = 512
HEADS = 8
HDIM = 64
BLK = 128
NB = 8
NBLK = 512
NODES = 65536
N_DOM = 64


def draw_matchings(key, part):
    key_sigma = jax.random.fold_in(key, 11)
    key_perm = jax.random.fold_in(key, 12)
    sigma = jax.random.permutation(key_sigma, N_DOM)
    perm_keys = jax.random.split(key_perm, N_DOM * 4)
    perms = jax.vmap(lambda one_key: jax.random.permutation(one_key, NB))(perm_keys).reshape(N_DOM, 4, NB)
    shape = (N_DOM, 4, NB)
    virtual = jnp.broadcast_to(jnp.arange(N_DOM)[:, None, None], shape)
    set_ids = jnp.broadcast_to(jnp.arange(4)[None, :, None], shape)
    rank_ids = jnp.broadcast_to(jnp.arange(NB)[None, None, :], shape)
    offset = (set_ids * NB + rank_ids) % N_DOM
    other = jnp.bitwise_xor(virtual, offset)
    own_dev = sigma[virtual]
    other_dev = sigma[other]
    own_blk = perms[own_dev, set_ids, rank_ids]
    other_blk = perms[other_dev, set_ids, rank_ids]
    source = (own_dev * NB + own_blk).astype(jnp.int32)
    target = (other_dev * NB + other_blk).astype(jnp.int32)
    result = jnp.zeros((4, NBLK), jnp.int32).at[set_ids, source].set(target)
    return result


def draw_edge_bias(key, part):
    key_base = jax.random.fold_in(key, 21)
    shape = (HEADS, 7, NODES)
    base = jnp.clip(1.5 * jax.random.normal(key_base, shape, jnp.float32), -9.0, 9.0)
    return base


def with_ends(values, key, low, top_value):
    longest = values.shape.index(max(values.shape))
    spots = []
    for shift in (0, 1):
        where = [jax.random.randint(jax.random.fold_in(key, axis), (), 0, length) for axis, length in enumerate(values.shape)]
        where[longest] = (where[longest] + shift) % values.shape[longest]
        spots.append(tuple(where))
    return values.at[spots[0]].set(low).at[spots[1]].set(top_value)


def with_spikes(drawn, stream_key, source, target, parts, factor):
    owner, partner = [(jnp.arange(drawn.shape[axis_at]) // (drawn.shape[axis_at] // parts)).reshape([-1 if axis == axis_at else 1 for axis in range(drawn.ndim)]) for axis_at in (source, target)]
    chosen = jax.random.permutation(stream_key, parts)[partner]
    strong = (owner == chosen) | (owner == (partner + parts // 2) % parts)
    return jnp.where(strong, factor * drawn, drawn)


def shard_levels(key, extent, shards, smallest, high):
    loudness, own = 1.0, jax.random.fold_in(key, 6)
    for axis_at, parts in shards:
        draws = jnp.exp(jax.random.uniform(jax.random.fold_in(own, axis_at), (parts,), jnp.float32, smallest / len(shards), high / len(shards)))
        loudness = loudness * jnp.repeat(draws, extent[axis_at] // parts).reshape([-1 if axis == axis_at else 1 for axis in range(len(extent))])
    return loudness


def bell_draw(key, shape, width, bound, cuts=(), kind=jnp.bfloat16):
    factor_of = shard_levels(key, shape, cuts, -0.22, 0.18) if cuts else 1.0
    drawn = jax.random.normal(key, shape, jnp.float32) * width * factor_of
    return jnp.minimum(jnp.maximum(drawn, -bound), bound).astype(kind)


def bell_draw_with(rng, dims, spread, most, shards, heavy, kind=jnp.bfloat16):
    values = spread * jax.random.normal(rng, dims, jnp.float32)
    if shards:
        values = values * shard_levels(rng, dims, shards, -0.22, 0.18)
    return jnp.clip(with_spikes(values, jax.random.fold_in(rng, 3), *heavy), -most, most).astype(kind)


def setup_inputs(seed: int = 0) -> dict:
    key_list = jax.random.split(jax.random.key(seed), 9)
    return {
        "features": bell_draw_with(key_list[0], (NODES, D), 1.0, 16.0, ((0, 64),), (0, 1, 64, 4.0)),
        "norm_gain": jnp.clip(1.0 + 0.15 * jax.random.normal(key_list[1], (D,), jnp.float32), 0.25, 1.75),
        "qkv_weight": bell_draw(key_list[2], (3, D, D), D ** -0.5, 0.25, ((2, 4),)),
        "out_weight": bell_draw(key_list[3], (D, D), (D // 16) ** -0.5, 1.0, ((1, 4),)),
        "edge_bias": draw_edge_bias(jax.random.fold_in(key_list[8], 71), 0),
        "band_mask": with_ends((jax.random.randint(key_list[5], (2, NBLK), 0, 3) < 2).astype(jnp.int32), jax.random.fold_in(key_list[5], 1), 0, 1),
        "matchings": draw_matchings(jax.random.fold_in(key_list[8], 71), 0),
        "cotangent": bell_draw_with(key_list[7], (NODES, D), 1.0, 16.0, ((0, 64),), (0, 1, 64, 4.0)),
    }


epsilon_norm = 1e-06
masked_score = -1e+30

def with_slots(blockwise, matchings):
    zero_row = jnp.zeros_like(blockwise[:1])
    left_side = jnp.concatenate([zero_row, blockwise[:-1]], axis=0)
    right_side = jnp.concatenate([blockwise[1:], zero_row], axis=0)
    partners = blockwise[matchings]
    return jnp.concatenate([left_side[None], blockwise[None], right_side[None], partners], axis=0)

def back_slots(slot_grad, matchings):
    total_grad = slot_grad[1]
    total_grad = total_grad.at[:-1].add(slot_grad[0][1:])
    total_grad = total_grad.at[1:].add(slot_grad[2][:-1])
    for which in range(4):
        total_grad = total_grad.at[matchings[which]].add(slot_grad[3 + which])
    return total_grad

def reference(features, norm_gain, qkv_weight, out_weight, edge_bias, band_mask, matchings, cotangent):
    score_scale = 1.0 / math.sqrt(HDIM)
    grad_scale = 1.0 / math.sqrt(NODES)
    feat_f32 = features.astype(jnp.float32)
    inv_rms = lax.rsqrt(lax.optimization_barrier(jnp.mean(feat_f32 * feat_f32, axis=1, keepdims=True)) + epsilon_norm)
    normed = (feat_f32 * inv_rms * norm_gain).astype(jnp.bfloat16)
    projected = [jnp.dot(normed, qkv_weight[proj_idx], preferred_element_type=jnp.float32).astype(jnp.bfloat16) for proj_idx in range(3)]
    d_attn = jnp.dot(cotangent, out_weight, preferred_element_type=jnp.float32).astype(jnp.bfloat16)
    block_ids = jnp.arange(NBLK)
    always = jnp.ones((NBLK,), dtype=bool)
    slot_valid = jnp.stack([(band_mask[0] == 1) & (block_ids > 0), always, (band_mask[1] == 1) & (block_ids < NBLK - 1), always, always, always, always])

    def per_head(head_num):
        start = (head_num * HDIM).astype(jnp.int32)

        def cut(matrix):
            return lax.dynamic_slice_in_dim(matrix, start, HDIM, 1).reshape(NBLK, BLK, HDIM)
        queries = cut(projected[0])
        keys_h = cut(projected[1])
        values_h = cut(projected[2])
        d_heads = cut(d_attn)
        head_bias = lax.dynamic_index_in_dim(edge_bias, head_num, 0, keepdims=False).reshape(7, NBLK, BLK)
        slot_keys = with_slots(keys_h, matchings).astype(jnp.float32)
        slot_values = with_slots(values_h, matchings).astype(jnp.float32)
        queries_f = queries.astype(jnp.float32)
        d_heads_f = d_heads.astype(jnp.float32)
        scores = jnp.einsum('bqe,sbke->sbqk', queries_f, slot_keys) * score_scale + head_bias[..., None]
        scores = jnp.where(slot_valid[:, :, None, None], scores, masked_score)
        row_peak = lax.optimization_barrier(jnp.max(scores, axis=(0, 3)))
        summed = lax.optimization_barrier(jnp.sum(jnp.exp(scores - row_peak[None, :, :, None]), axis=(0, 3)))
        logsum = row_peak + jnp.log(summed)
        prob_full = jnp.exp(scores - logsum[None, :, :, None])
        prob_half = prob_full.astype(jnp.bfloat16)
        attended = jnp.einsum('sbqk,sbke->bqe', prob_half.astype(jnp.float32), slot_values).astype(jnp.bfloat16)
        delta_rows = lax.optimization_barrier(jnp.sum(d_heads_f * attended.astype(jnp.float32), axis=-1))
        d_prob = jnp.einsum('bqe,sbke->sbqk', d_heads_f, slot_values)
        d_score = (prob_full * (d_prob - delta_rows[None, :, :, None])).astype(jnp.bfloat16)
        d_score_f = d_score.astype(jnp.float32)
        d_query = (score_scale * jnp.einsum('sbqk,sbke->bqe', d_score_f, slot_keys)).astype(jnp.bfloat16)
        key_slots = score_scale * jnp.einsum('sbqk,bqe->sbke', d_score_f, queries_f)
        value_slots = jnp.einsum('sbqk,bqe->sbke', prob_half.astype(jnp.float32), d_heads_f)
        d_key = back_slots(key_slots, matchings).astype(jnp.bfloat16)
        d_value = back_slots(value_slots, matchings).astype(jnp.bfloat16)
        return (attended, d_query, d_key, d_value)
    stacked = lax.map(per_head, jnp.arange(HEADS, dtype=jnp.int32))

    def merge_heads(per_heads):
        return per_heads.transpose(1, 2, 0, 3).reshape(NODES, D)
    attended = merge_heads(stacked[0])
    d_proj = [merge_heads(stacked[1]), merge_heads(stacked[2]), merge_heads(stacked[3])]
    layer_out = (feat_f32 + jnp.dot(attended, out_weight.T, preferred_element_type=jnp.float32)).astype(jnp.bfloat16)
    grad_out = jnp.dot(cotangent.T, attended, preferred_element_type=jnp.float32) * grad_scale
    grad_qkv = jnp.stack([jnp.dot(normed.T, d_proj[proj_idx], preferred_element_type=jnp.float32) for proj_idx in range(3)]) * grad_scale
    d_normed = jnp.dot(d_proj[0], qkv_weight[0].T, preferred_element_type=jnp.float32)
    d_normed = d_normed + jnp.dot(d_proj[1], qkv_weight[1].T, preferred_element_type=jnp.float32)
    d_normed = d_normed + jnp.dot(d_proj[2], qkv_weight[2].T, preferred_element_type=jnp.float32)
    row_dot = lax.optimization_barrier(jnp.sum(d_normed * norm_gain * feat_f32, axis=1, keepdims=True))
    grad_input = (cotangent.astype(jnp.float32) + inv_rms * norm_gain * d_normed - feat_f32 * inv_rms * inv_rms * inv_rms * row_dot / D).astype(jnp.bfloat16)
    return (layer_out, grad_input, grad_qkv, grad_out)
```

```python
import math

import jax
import jax.numpy as jnp
from jax import lax
from jax.sharding import PartitionSpec as P

epsilon_norm = 1e-06
masked_score = -1e30
bf16 = jnp.bfloat16
f32 = jnp.float32


def head_sum(partial, extra):
    count = lax.axis_size("head")
    here = lax.axis_index("head")
    cols = partial.shape[1] // count

    def chunk(step):
        piece = lax.dynamic_slice_in_dim(partial, ((here + step) % count) * cols, cols, 1)
        return piece

    own = chunk(0).astype(f32)
    total_extra = extra
    for step in range(1, count):
        piece = chunk(step).astype(bf16)
        if extra is not None:
            high = lax.reduce_precision(extra, 8, 7)
            piece = jnp.concatenate([piece, high.astype(bf16), (extra - high).astype(bf16)], axis=0)
        got = lax.ppermute(piece, "head", [(i, (i + step) % count) for i in range(count)])
        rows = partial.shape[0]
        own = own + got[:rows].astype(f32)
        if extra is not None:
            more = extra.shape[0]
            total_extra = (
                total_extra
                + got[rows : rows + more].astype(f32)
                + got[rows + more :].astype(f32)
            )
    return own, total_extra


def shift_dom(x, step):
    count = lax.axis_size("dom")
    pairs = [(i, i + step) for i in range(count) if 0 <= i + step < count]
    return lax.ppermute(x, "dom", pairs)


def body(features, norm_gain, qkv_weight, out_weight, edge_bias, band_mask, matchings, cotangent):
    row_count, model_width = features.shape
    local_cols = qkv_weight.shape[2]
    heads_here = edge_bias.shape[0]
    head_size = local_cols // heads_here
    blocks = band_mask.shape[1]
    block_len = row_count // blocks
    dom_size = lax.axis_size("dom")
    dom_index = lax.axis_index("dom")
    head_index = lax.axis_index("head")
    score_scale = 1.0 / math.sqrt(head_size)
    grad_scale = 1.0 / math.sqrt(dom_size * row_count)
    slots_all = 4 * blocks
    pair_cols = 2 * local_cols
    grad_rows = model_width // dom_size
    feat_f32 = features.astype(f32)
    inv_rms = lax.rsqrt(jnp.mean(feat_f32 * feat_f32, axis=1, keepdims=True) + epsilon_norm)
    normed = (feat_f32 * inv_rms * norm_gain).astype(bf16)
    projected = jnp.einsum(
        "rd,tdc->trc", normed, qkv_weight, preferred_element_type=f32
    ).astype(bf16)
    queries = projected[0].reshape(blocks, block_len, heads_here, head_size)
    keyval = jnp.concatenate([projected[1], projected[2]], axis=1).reshape(
        blocks, block_len, pair_cols
    )
    target = (matchings // blocks).reshape(slots_all)
    item_ids = jnp.arange(slots_all, dtype=jnp.int32)
    devices = jnp.arange(dom_size, dtype=jnp.int32)
    at_send = jnp.sum(jnp.where(target[None, :] == devices[:, None], item_ids[None, :], 0), axis=1)
    outgoing = keyval[at_send % blocks]
    incoming = lax.all_to_all(outgoing, "dom", split_axis=0, concat_axis=0, tiled=True)
    before = shift_dom(keyval[-1:], 1)
    after = shift_dom(keyval[:1], -1)
    rimmed = jnp.concatenate([before, keyval, after], axis=0)
    far_keyval = incoming[target].reshape(4, blocks, block_len, pair_cols)
    slot_data = jnp.concatenate(
        [rimmed[None, :-2], keyval[None], rimmed[None, 2:], far_keyval], axis=0
    )
    slot_keys = slot_data[..., :local_cols].reshape(7, blocks, block_len, heads_here, head_size)
    slot_values = slot_data[..., local_cols:].reshape(7, blocks, block_len, heads_here, head_size)
    global_blk = dom_index * blocks + jnp.arange(blocks, dtype=jnp.int32)
    left_ok = (band_mask[0] == 1) & (global_blk > 0)
    right_ok = (band_mask[1] == 1) & (global_blk < dom_size * blocks - 1)
    always = jnp.ones((blocks,), dtype=bool)
    slot_valid = jnp.stack([left_ok, always, right_ok, always, always, always, always])
    bias_blocks = edge_bias.reshape(heads_here, 7, blocks, block_len)
    masked_bias = jnp.where(slot_valid[None, :, :, None], bias_blocks, masked_score)
    scores = (
        jnp.einsum("bqhe,sbkhe->hsbqk", queries, slot_keys, preferred_element_type=f32)
        * score_scale
        + masked_bias[..., None]
    )
    row_peak = jnp.max(scores, axis=(1, 4))
    summed = jnp.sum(jnp.exp(scores - row_peak[:, None, :, :, None]), axis=(1, 4))
    logsum = row_peak + jnp.log(summed)
    prob_full = jnp.exp(scores - logsum[:, None, :, :, None])
    prob_half = prob_full.astype(bf16)
    att_heads = jnp.einsum(
        "hsbqk,sbkhe->bqhe", prob_half, slot_values, preferred_element_type=f32
    ).astype(bf16)
    attended = att_heads.reshape(row_count, local_cols)
    partial_out = lax.dot_general(
        attended, out_weight, (((1,), (1,)), ((), ())), preferred_element_type=f32
    )
    summed_out, _ = head_sum(partial_out, None)
    own_feat = lax.dynamic_slice_in_dim(features, head_index * local_cols, local_cols, 1).astype(f32)
    layer_out = (summed_out + own_feat).astype(bf16)
    d_attn = jnp.dot(cotangent, out_weight, preferred_element_type=f32).astype(bf16)
    grad_out_part = (
        lax.dot_general(cotangent, attended, (((0,), (0,)), ((), ())), preferred_element_type=f32)
        * grad_scale
    )
    d_heads = d_attn.reshape(blocks, block_len, heads_here, head_size)
    delta_rows = jnp.sum(d_heads.astype(f32) * att_heads.astype(f32), axis=3).transpose(2, 0, 1)
    d_prob = jnp.einsum("bqhe,sbkhe->hsbqk", d_heads, slot_values, preferred_element_type=f32)
    d_score = (prob_full * (d_prob - delta_rows[:, None, :, :, None])).astype(bf16)
    d_query = (
        (
            score_scale
            * jnp.einsum("hsbqk,sbkhe->bqhe", d_score, slot_keys, preferred_element_type=f32)
        )
        .astype(bf16)
        .reshape(row_count, local_cols)
    )
    grad_q_part = (
        lax.dot_general(normed, d_query, (((0,), (0,)), ((), ())), preferred_element_type=f32)
        * grad_scale
    )

    def key_grads(score_grad, prob_part):
        count = score_grad.shape[1]
        key_grad = score_scale * jnp.einsum(
            "hsbqk,bqhe->sbkhe", score_grad, queries, preferred_element_type=f32
        )
        val_grad = jnp.einsum("hsbqk,bqhe->sbkhe", prob_part, d_heads, preferred_element_type=f32)
        return jnp.concatenate(
            [
                key_grad.reshape(count, blocks, block_len, local_cols),
                val_grad.reshape(count, blocks, block_len, local_cols),
            ],
            axis=-1,
        )

    far_grads = (
        key_grads(d_score[:, 3:], prob_half[:, 3:])
        .astype(bf16)
        .reshape(slots_all, block_len, pair_cols)
    )
    riders = (
        jnp.concatenate([grad_out_part, grad_q_part], axis=1)
        .reshape(dom_size, grad_rows, pair_cols)
        .astype(bf16)
    )
    returned = lax.all_to_all(
        jnp.concatenate([far_grads[at_send], riders], axis=1),
        "dom",
        split_axis=0,
        concat_axis=0,
        tiled=True,
    )
    near_grads = key_grads(d_score[:, :3], prob_half[:, :3])
    zero_block = jnp.zeros_like(near_grads[0][:1])
    rim_left = shift_dom(near_grads[0][:1].astype(bf16), -1).astype(f32)
    rim_right = shift_dom(near_grads[2][-1:].astype(bf16), 1).astype(f32)
    own_grads = (
        near_grads[1]
        + jnp.concatenate([near_grads[0][1:], rim_left], axis=0)
        + jnp.concatenate([rim_right, near_grads[2][:-1]], axis=0)
    )
    grads_oq = jnp.sum(returned[:, block_len:].astype(f32), axis=0)
    back = returned[:, :block_len][target].reshape(4, blocks, block_len, pair_cols).astype(f32)
    own_grads = (own_grads + jnp.sum(back, axis=0)).astype(bf16).reshape(row_count, pair_cols)
    grad_kv_part = (
        lax.dot_general(normed, own_grads, (((0,), (0,)), ((), ())), preferred_element_type=f32)
        * grad_scale
    )
    grads_kv = jnp.sum(
        lax.all_to_all(
            grad_kv_part.reshape(dom_size, grad_rows, pair_cols).astype(bf16),
            "dom",
            split_axis=0,
            concat_axis=0,
            tiled=True,
        ).astype(f32),
        axis=0,
    )
    grad_out = grads_oq[:, :local_cols]
    grad_qkv = jnp.stack([grads_oq[:, local_cols:], grads_kv[:, :local_cols], grads_kv[:, local_cols:]])
    d_proj = jnp.concatenate([d_query, own_grads], axis=1)
    weights = qkv_weight.transpose(1, 0, 2).reshape(model_width, 3 * local_cols)
    d_normed = lax.dot_general(
        d_proj, weights, (((1,), (1,)), ((), ())), preferred_element_type=f32
    )
    row_part = jnp.sum(d_normed * norm_gain * feat_f32, axis=1).reshape(row_count // 128, 128)
    share_grad, row_dot = head_sum(d_normed, row_part)
    row_dot = row_dot.reshape(row_count, 1)
    own_gain = lax.dynamic_slice_in_dim(norm_gain, head_index * local_cols, local_cols, 0)
    own_cot = lax.dynamic_slice_in_dim(cotangent, head_index * local_cols, local_cols, 1).astype(f32)
    grad_input = (
        own_cot
        + inv_rms * own_gain * share_grad
        - own_feat * inv_rms * inv_rms * inv_rms * row_dot / model_width
    ).astype(bf16)
    return (layer_out, grad_input, grad_qkv, grad_out)


def solution(mesh):
    in_specs = (
        P("dom", None),
        P(),
        P(None, None, "head"),
        P(None, "head"),
        P("head", None, "dom"),
        P(None, "dom"),
        P(None, "dom"),
        P("dom", None),
    )
    out_specs = (P("dom", "head"), P("dom", "head"), P(None, "dom", "head"), P("dom", "head"))
    return jax.shard_map(body, mesh=mesh, in_specs=in_specs, out_specs=out_specs, check_vma=False)
```

```python
import math

import jax
import jax.numpy as jnp
from jax import lax
from jax.experimental import pallas as pl
from jax.experimental.pallas import tpu as pltpu
from jax.sharding import PartitionSpec as P

epsilon_norm = 1e-06
masked_score = -1e30
bf16 = jnp.bfloat16
f32 = jnp.float32
vmem = pl.BlockSpec(memory_space=pltpu.VMEM)
smem = pl.BlockSpec(memory_space=pltpu.SMEM)
NN = (((1,), (0,)), ((), ()))
NT = (((1,), (1,)), ((), ()))
TN = (((0,), (0,)), ((), ()))


def mm(a, b, dims):
    return lax.dot_general(a, b, dims, preferred_element_type=f32)


def pack_call(matchings, features, gain, qkv_weight, dom_size):
    sets, blocks = matchings.shape
    rows, width = features.shape
    cols = qkv_weight.shape[2]
    block_len = rows // blocks

    def kernel(match_ref, feat_ref, gain_ref, w_ref, slots_ref, kv_ref, normed_ref, inv_ref):
        weight = jnp.concatenate([w_ref[1], w_ref[2]], axis=1)

        @pl.loop(0, blocks)
        def _(b):
            at = pl.ds(pl.multiple_of(b * block_len, block_len), block_len)
            x = feat_ref[at, :].astype(f32)
            inv = lax.rsqrt(jnp.mean(x * x, axis=1, keepdims=True) + epsilon_norm)
            normed = (x * inv * gain_ref[...]).astype(bf16)
            normed_ref[at, :] = normed
            inv_ref[at, :] = inv
            kv = mm(normed, weight, NN).astype(bf16)
            kv_ref[b] = kv
            for j in range(sets):
                slots_ref[match_ref[j, b] // blocks] = kv

    return pl.pallas_call(
        kernel,
        out_shape=(
            jax.ShapeDtypeStruct((dom_size, block_len, 2 * cols), bf16),
            jax.ShapeDtypeStruct((blocks, block_len, 2 * cols), bf16),
            jax.ShapeDtypeStruct((rows, width), bf16),
            jax.ShapeDtypeStruct((rows, 1), f32),
        ),
        in_specs=[smem, vmem, vmem, vmem],
        out_specs=(vmem, vmem, vmem, vmem),
        name="pack_slots",
    )(matchings, features, gain, qkv_weight)


def attention_call(matchings, queries2, d_attn2, bias, rimmed, incoming, score_scale):
    sets, blocks = matchings.shape
    slots = sets + 3
    dom_size, block_len, pair = incoming.shape
    cols = pair // 2
    wide = queries2.shape[1]

    def kernel(match_ref, q_ref, do_ref, bias_ref, rim_ref, in_ref, out_ref, near_ref, att_ref, dq_ref):
        near_ref[...] = jnp.zeros_like(near_ref)
        half = lax.broadcasted_iota(jnp.int32, (block_len, cols), 1) < cols // 2

        @pl.loop(0, blocks)
        def _(b):
            q2 = q_ref[b]
            do2 = do_ref[b]
            partner = [match_ref[j, b] // blocks for j in range(sets)]
            kv = [rim_ref[b + s] for s in range(3)] + [in_ref[t] for t in partner]
            score = [
                mm(kv[s][:, :cols], q2, NT) * score_scale + bias_ref[b, pl.ds(s, 1), :]
                for s in range(slots)
            ]
            peak = score[0].max(axis=0, keepdims=True)
            for s in range(1, slots):
                peak = jnp.maximum(peak, score[s].max(axis=0, keepdims=True))
            weight = [jnp.exp(x - peak) for x in score]
            total = weight[0].sum(axis=0, keepdims=True)
            for s in range(1, slots):
                total = total + weight[s].sum(axis=0, keepdims=True)
            share = 1.0 / total
            prob = [x * share for x in weight]
            prob_half = [x.astype(bf16) for x in prob]
            d_prob = [mm(kv[s][:, cols:], do2, NT) for s in range(slots)]
            delta = jnp.zeros((1, wide), f32)
            for s in range(slots):
                delta = delta + (prob_half[s].astype(f32) * d_prob[s]).sum(axis=0, keepdims=True)
            d_score = [(prob[s] * (d_prob[s] - delta)).astype(bf16) for s in range(slots)]
            att = mm(prob_half[0], kv[0][:, cols:], TN)
            d_query = mm(d_score[0], kv[0][:, :cols], TN)
            for s in range(1, slots):
                att = att + mm(prob_half[s], kv[s][:, cols:], TN)
                d_query = d_query + mm(d_score[s], kv[s][:, :cols], TN)
            att_ref[b] = jnp.where(half, att[:block_len], att[block_len:]).astype(bf16)
            dq_ref[b] = (jnp.where(half, d_query[:block_len], d_query[block_len:]) * score_scale).astype(bf16)
            for s in range(slots):
                d_key = mm(d_score[s], q2, NN) * score_scale
                d_value = mm(prob_half[s], do2, NN)
                if s < 3:
                    near_ref[b + s, :, :cols] += d_key
                    near_ref[b + s, :, cols:] += d_value
                else:
                    out_ref[partner[s - 3], :, :cols] = d_key.astype(bf16)
                    out_ref[partner[s - 3], :, cols:] = d_value.astype(bf16)

    return pl.pallas_call(
        kernel,
        out_shape=(
            jax.ShapeDtypeStruct((dom_size, block_len, pair), bf16),
            jax.ShapeDtypeStruct((blocks + 2, block_len, pair), f32),
            jax.ShapeDtypeStruct((blocks, block_len, cols), bf16),
            jax.ShapeDtypeStruct((blocks, block_len, cols), bf16),
        ),
        in_specs=[smem, vmem, vmem, vmem, vmem, vmem],
        out_specs=(vmem, vmem, vmem, vmem),
        name="attention",
    )(matchings, queries2, d_attn2, bias, rimmed, incoming)


def finish_call(
    matchings, returned, own, d_query, normed_t, weights, scaled_feat, riders, grad_scale, heads
):
    sets, blocks = matchings.shape
    dom_size, block_len, pair = returned.shape
    cols = pair // 2
    rows = blocks * block_len
    width = normed_t.shape[0]
    peers = heads - 1

    def kernel(
        match_ref, back_ref, own_ref, dq_ref, nt_ref, w_ref, sf_ref, ride_ref,
        gkv_ref, pay_ref, mine_ref, dot_ref, dproj_ref,
    ):
        @pl.loop(0, blocks)
        def _(b):
            at = pl.ds(pl.multiple_of(b * block_len, block_len), block_len)
            total = own_ref[b]
            for j in range(sets):
                total = total + back_ref[match_ref[j, b] // blocks].astype(f32)
            d_proj = jnp.concatenate([dq_ref[at, :], total.astype(bf16)], axis=1)
            dproj_ref[at, :] = d_proj
            d_normed = mm(d_proj, w_ref[...], NT)
            mine_ref[at, :] = d_normed[:, :cols]
            for k in range(peers):
                pay_ref[k, at, :] = d_normed[:, (k + 1) * cols : (k + 2) * cols].astype(bf16)
            lanes = d_normed[:, :cols] * sf_ref[at, :cols]
            for k in range(1, heads):
                part = slice(k * cols, (k + 1) * cols)
                lanes = lanes + d_normed[:, part] * sf_ref[at, part]
            dot_ref[pl.ds(b, 1), :] = lanes.T.sum(axis=0, keepdims=True)

        grads = mm(nt_ref[...], dproj_ref[:, cols:], NN) * grad_scale
        gkv_ref[:, :, :pair] = ride_ref[...]
        gkv_ref[:, :, pair:] = grads.reshape(dom_size, width // dom_size, pair).astype(bf16)
        high = dot_ref[...].astype(bf16)
        low = dot_ref[...] - high.astype(f32)
        tail = jnp.concatenate([high.astype(f32), low], axis=0).astype(bf16)
        for k in range(peers):
            pay_ref[k, rows:, :] = tail

    return pl.pallas_call(
        kernel,
        out_shape=(
            jax.ShapeDtypeStruct((dom_size, width // dom_size, 2 * pair), bf16),
            jax.ShapeDtypeStruct((peers, rows + 2 * blocks, cols), bf16),
            jax.ShapeDtypeStruct((rows, cols), f32),
            jax.ShapeDtypeStruct((blocks, cols), f32),
        ),
        in_specs=[smem] + [vmem] * 7,
        out_specs=(vmem, vmem, vmem, vmem),
        scratch_shapes=[pltpu.VMEM((rows, 3 * cols), bf16)],
        name="finish",
    )(matchings, returned, own, d_query, normed_t, weights, scaled_feat, riders)


def ring(x, axis, step):
    count = lax.axis_size(axis)
    return lax.ppermute(x, axis, [(i, (i + step) % count) for i in range(count)])


def shift_dom(x, step):
    count = lax.axis_size("dom")
    pairs = [(i, i + step) for i in range(count) if 0 <= i + step < count]
    return lax.ppermute(x, "dom", pairs)


def spread(x):
    return lax.all_to_all(x, "dom", split_axis=0, concat_axis=0, tiled=True)


def body(features, norm_gain, qkv_weight, out_weight, edge_bias, band_mask, matchings, cotangent):
    row_count, model_width = features.shape
    local_cols = qkv_weight.shape[2]
    heads_here = edge_bias.shape[0]
    head_size = local_cols // heads_here
    blocks = band_mask.shape[1]
    block_len = row_count // blocks
    dom_size = lax.axis_size("dom")
    dom_index = lax.axis_index("dom")
    head_count = lax.axis_size("head")
    head_index = lax.axis_index("head")
    score_scale = 1.0 / math.sqrt(head_size)
    grad_scale = 1.0 / math.sqrt(dom_size * row_count)
    grad_rows = model_width // dom_size
    pair_cols = 2 * local_cols

    def rolled(x, axis):
        both = jnp.concatenate([x, x], axis=axis)
        return lax.dynamic_slice_in_dim(both, head_index * local_cols, model_width, axis)

    outgoing, keyval, normed, inv_rms = pack_call(
        matchings, features, norm_gain.reshape(1, model_width), qkv_weight, dom_size
    )
    incoming = spread(outgoing)
    before = shift_dom(keyval[-1:], 1)
    after = shift_dom(keyval[:1], -1)
    rimmed = jnp.concatenate([before, keyval, after], axis=0)

    def both_heads(x):
        x = x.reshape(blocks, block_len, local_cols)
        lane = lax.broadcasted_iota(jnp.int32, (1, 1, local_cols), 2) // head_size
        zero = jnp.zeros((), x.dtype)
        return jnp.concatenate([jnp.where(lane == h, x, zero) for h in range(heads_here)], axis=1)

    queries2 = both_heads(jnp.dot(normed, qkv_weight[0], preferred_element_type=f32).astype(bf16))
    d_attn2 = both_heads(jnp.dot(cotangent, out_weight, preferred_element_type=f32).astype(bf16))
    global_blk = dom_index * blocks + jnp.arange(blocks, dtype=jnp.int32)
    left_ok = (band_mask[0] == 1) & (global_blk > 0)
    right_ok = (band_mask[1] == 1) & (global_blk < dom_size * blocks - 1)
    always = jnp.ones((blocks,), dtype=bool)
    slot_valid = jnp.stack([left_ok, always, right_ok, always, always, always, always])
    bias_blocks = edge_bias.reshape(heads_here, 7, blocks, block_len)
    masked_bias = jnp.where(slot_valid[None, :, :, None], bias_blocks, masked_score)
    masked_bias = masked_bias.transpose(2, 1, 0, 3).reshape(blocks, 7, heads_here * block_len)
    far_grads, near, attended, d_query = attention_call(
        matchings, queries2, d_attn2, masked_bias, rimmed, incoming, score_scale
    )
    returned = spread(far_grads)
    attended = attended.reshape(row_count, local_cols)
    d_query = d_query.reshape(row_count, local_cols)
    rim_left = shift_dom(near[:1].astype(bf16), -1)
    rim_right = shift_dom(near[-1:].astype(bf16), 1)
    own_grads = jnp.concatenate(
        [
            near[1:2] + rim_right.astype(f32),
            near[2:-2],
            near[-2:-1] + rim_left.astype(f32),
        ],
        axis=0,
    )
    grad_out_part = lax.dot_general(
        cotangent, attended, (((0,), (0,)), ((), ())), preferred_element_type=f32
    )
    grad_q_part = lax.dot_general(
        normed, d_query, (((0,), (0,)), ((), ())), preferred_element_type=f32
    )
    riders = jnp.concatenate([grad_out_part * grad_scale, grad_q_part * grad_scale], axis=1)
    riders = riders.astype(bf16).reshape(dom_size, grad_rows, pair_cols)
    partial_out = lax.dot_general(
        attended, rolled(out_weight, 0), (((1,), (1,)), ((), ())), preferred_element_type=f32
    )
    own_feat = lax.dynamic_slice_in_dim(features, head_index * local_cols, local_cols, 1).astype(f32)
    layer_sum = partial_out[:, :local_cols]
    for step in range(1, head_count):
        piece = partial_out[:, step * local_cols : (step + 1) * local_cols].astype(bf16)
        layer_sum = layer_sum + ring(piece, "head", step).astype(f32)
    layer_out = (layer_sum + own_feat).astype(bf16)
    weights = qkv_weight.transpose(1, 0, 2).reshape(model_width, 3 * local_cols)
    scaled_feat = rolled(features.astype(f32) * norm_gain, 1)
    grads, payload, share_grad, row_dot = finish_call(
        matchings, returned, own_grads, d_query, normed.T, rolled(weights, 0), scaled_feat,
        riders, grad_scale, head_count,
    )
    for step in range(1, head_count):
        got = ring(payload[step - 1], "head", step).astype(f32)
        share_grad = share_grad + got[:row_count]
        row_dot = row_dot + got[row_count : row_count + blocks] + got[row_count + blocks :]
    grads = jnp.sum(spread(grads).astype(f32), axis=0)
    grad_out, grad_query, grad_key, grad_value = jnp.split(grads, 4, axis=1)
    grad_qkv = jnp.stack([grad_query, grad_key, grad_value])
    row_dot = row_dot.reshape(row_count, 1)
    own_gain = lax.dynamic_slice_in_dim(norm_gain, head_index * local_cols, local_cols, 0)
    own_cot = lax.dynamic_slice_in_dim(cotangent, head_index * local_cols, local_cols, 1).astype(f32)
    grad_input = (
        own_cot
        + inv_rms * own_gain * share_grad
        - own_feat * inv_rms * inv_rms * inv_rms * row_dot / model_width
    ).astype(bf16)
    return (layer_out, grad_input, grad_qkv, grad_out)


def solution(mesh):
    in_specs = (
        P("dom", None),
        P(),
        P(None, None, "head"),
        P(None, "head"),
        P("head", None, "dom"),
        P(None, "dom"),
        P(None, "dom"),
        P("dom", None),
    )
    out_specs = (P("dom", "head"), P("dom", "head"), P(None, "dom", "head"), P("dom", "head"))
    return jax.shard_map(body, mesh=mesh, in_specs=in_specs, out_specs=out_specs, check_vma=False)
```

```python
import math

import jax
import jax.numpy as jnp
from jax import lax
from jax.experimental import pallas as pl
from jax.experimental.pallas import tpu as pltpu
from jax.sharding import PartitionSpec as P

epsilon_norm = 1e-06
masked_score = -1e30
bf16 = jnp.bfloat16
f32 = jnp.float32
vmem = pl.BlockSpec(memory_space=pltpu.VMEM)
hbm = pl.BlockSpec(memory_space=pl.ANY)
smem = pl.BlockSpec(memory_space=pltpu.SMEM)
NN = (((1,), (0,)), ((), ()))
NT = (((1,), (1,)), ((), ()))
TN = (((0,), (0,)), ((), ()))


def mm(a, b, dims):
    return lax.dot_general(a, b, dims, preferred_element_type=f32)


def pack_call(matchings, features, gain, qkv_weight, dom_size):
    sets, blocks = matchings.shape
    rows, width = features.shape
    cols = qkv_weight.shape[2]
    block_len = rows // blocks

    def kernel(match_ref, feat_ref, gain_ref, w_ref, slots_ref, kv_ref, normed_ref, inv_ref, sems):
        weight = jnp.concatenate([w_ref[1], w_ref[2]], axis=1)

        def send(b, j):
            slot = slots_ref.at[match_ref[j, b] // blocks]
            return pltpu.make_async_copy(kv_ref.at[b], slot, sems.at[b * sets + j])

        @pl.loop(0, blocks)
        def _(b):
            at = pl.ds(pl.multiple_of(b * block_len, block_len), block_len)
            x = feat_ref[at, :].astype(f32)
            inv = lax.rsqrt(jnp.mean(x * x, axis=1, keepdims=True) + epsilon_norm)
            normed = (x * inv * gain_ref[...]).astype(bf16)
            normed_ref[at, :] = normed
            inv_ref[at, :] = inv
            kv_ref[b] = mm(normed, weight, NN).astype(bf16)
            for j in range(sets):
                send(b, j).start()

        @pl.loop(0, blocks)
        def _(b):
            for j in range(sets):
                send(b, j).wait()

    return pl.pallas_call(
        kernel,
        out_shape=(
            jax.ShapeDtypeStruct((dom_size, block_len, 2 * cols), bf16),
            jax.ShapeDtypeStruct((blocks, block_len, 2 * cols), bf16),
            jax.ShapeDtypeStruct((rows, width), bf16),
            jax.ShapeDtypeStruct((rows, 1), f32),
        ),
        in_specs=[smem, vmem, vmem, vmem],
        out_specs=(hbm, vmem, vmem, vmem),
        scratch_shapes=[pltpu.SemaphoreType.DMA((sets * blocks,))],
        name="pack_slots",
    )(matchings, features, gain, qkv_weight)


def attention_call(matchings, queries2, d_attn2, bias, rimmed, incoming, score_scale):
    sets, blocks = matchings.shape
    slots = sets + 3
    dom_size, block_len, pair = incoming.shape
    cols = pair // 2

    def kernel(
        match_ref, q_ref, do_ref, bias_ref, rim_ref, in_ref,
        out_ref, near_ref, att_ref, dq_ref, far_ref, grad_ref, in_sems, out_sems,
    ):
        def fetch(b, j):
            slot = in_ref.at[match_ref[j, b] // blocks]
            at = b * sets + j
            return pltpu.make_async_copy(slot, far_ref.at[at], in_sems.at[at])

        def send(b, j):
            slot = out_ref.at[match_ref[j, b] // blocks]
            at = b * sets + j
            return pltpu.make_async_copy(grad_ref.at[at], slot, out_sems.at[at])

        @pl.loop(0, blocks)
        def _(b):
            for j in range(sets):
                fetch(b, j).start()

        near_ref[...] = jnp.zeros_like(near_ref)
        half = lax.broadcasted_iota(jnp.int32, (block_len, cols), 1) < cols // 2

        @pl.loop(0, blocks)
        def _(b):
            for j in range(sets):
                fetch(b, j).wait()
            q2 = q_ref[b]
            do2 = do_ref[b]
            kv = [rim_ref[b + s] for s in range(3)] + [far_ref[b * sets + j] for j in range(sets)]
            row_bias = [bias_ref[b, pl.ds(s, 1), :] for s in range(slots)]
            score = [mm(kv[s][:, :cols], q2, NT) for s in range(slots)]
            peak = score[0].max(axis=0, keepdims=True) + row_bias[0]
            for s in range(1, slots):
                peak = jnp.maximum(peak, score[s].max(axis=0, keepdims=True) + row_bias[s])
            weight = [jnp.exp(score[s] + (row_bias[s] - peak)) for s in range(slots)]
            total = weight[0].sum(axis=0, keepdims=True)
            for s in range(1, slots):
                total = total + weight[s].sum(axis=0, keepdims=True)
            share = 1.0 / total
            prob = [x * share for x in weight]
            prob_half = [x.astype(bf16) for x in prob]
            pull = [prob[s] * mm(kv[s][:, cols:], do2, NT) for s in range(slots)]
            delta = pull[0].sum(axis=0, keepdims=True)
            for s in range(1, slots):
                delta = delta + pull[s].sum(axis=0, keepdims=True)
            d_score = [(pull[s] - prob[s] * delta).astype(bf16) for s in range(slots)]
            att = mm(prob_half[0], kv[0][:, cols:], TN)
            d_query = mm(d_score[0], kv[0][:, :cols], TN)
            for s in range(1, slots):
                att = att + mm(prob_half[s], kv[s][:, cols:], TN)
                d_query = d_query + mm(d_score[s], kv[s][:, :cols], TN)
            att_ref[b] = jnp.where(half, att[:block_len], att[block_len:]).astype(bf16)
            dq_ref[b] = (
                jnp.where(half, d_query[:block_len], d_query[block_len:]) * score_scale
            ).astype(bf16)
            for s in range(slots):
                d_key = mm(d_score[s], q2, NN)
                d_value = mm(prob_half[s], do2, NN)
                if s < 3:
                    near_ref[b + s, :, :cols] += d_key
                    near_ref[b + s, :, cols:] += d_value
                else:
                    grad_ref[b * sets + s - 3, :, :cols] = d_key.astype(bf16)
                    grad_ref[b * sets + s - 3, :, cols:] = d_value.astype(bf16)
            for j in range(sets):
                send(b, j).start()

        @pl.loop(0, blocks)
        def _(b):
            for j in range(sets):
                send(b, j).wait()

    return pl.pallas_call(
        kernel,
        out_shape=(
            jax.ShapeDtypeStruct((dom_size, block_len, pair), bf16),
            jax.ShapeDtypeStruct((blocks + 2, block_len, pair), f32),
            jax.ShapeDtypeStruct((blocks, block_len, cols), bf16),
            jax.ShapeDtypeStruct((blocks, block_len, cols), bf16),
        ),
        in_specs=[smem, vmem, vmem, vmem, vmem, hbm],
        out_specs=(hbm, vmem, vmem, vmem),
        scratch_shapes=[
            pltpu.VMEM((sets * blocks, block_len, pair), bf16),
            pltpu.VMEM((sets * blocks, block_len, pair), bf16),
            pltpu.SemaphoreType.DMA((sets * blocks,)),
            pltpu.SemaphoreType.DMA((sets * blocks,)),
        ],
        name="attention",
    )(matchings, queries2, d_attn2, bias, rimmed, incoming)


def finish_call(
    matchings, returned, own, d_query, normed_t, weights, feat, gain, riders, grad_scale, heads
):
    sets, blocks = matchings.shape
    dom_size, block_len, pair = returned.shape
    cols = pair // 2
    rows = blocks * block_len
    width = normed_t.shape[0]
    peers = heads - 1

    def kernel(
        match_ref, back_ref, own_ref, dq_ref, nt_ref, w_ref, feat_ref, gain_ref, ride_ref,
        gkv_ref, mine_ref, dot_ref, *rest,
    ):
        pay_refs = rest[:peers]
        dproj_ref, buf_ref, sems = rest[peers:]

        def fetch(b, j):
            slot = back_ref.at[match_ref[j, b] // blocks]
            at = b * sets + j
            return pltpu.make_async_copy(slot, buf_ref.at[at], sems.at[at])

        @pl.loop(0, blocks)
        def _(b):
            for j in range(sets):
                fetch(b, j).start()

        @pl.loop(0, blocks)
        def _(b):
            at = pl.ds(pl.multiple_of(b * block_len, block_len), block_len)
            total = own_ref[b]
            for j in range(sets):
                fetch(b, j).wait()
                total = total + buf_ref[b * sets + j].astype(f32)
            d_proj = jnp.concatenate([dq_ref[at, :], total.astype(bf16)], axis=1)
            dproj_ref[at, :] = d_proj
            d_normed = mm(d_proj, w_ref[...], NT)
            mine_ref[at, :] = d_normed[:, :cols]
            for k in range(peers):
                pay_refs[k][at, :] = d_normed[:, (k + 1) * cols : (k + 2) * cols].astype(bf16)
            moved = d_normed * (feat_ref[at, :].astype(f32) * gain_ref[...])
            lanes = moved[:, :cols]
            for k in range(1, heads):
                lanes = lanes + moved[:, k * cols : (k + 1) * cols]
            dot_ref[pl.ds(b, 1), :] = lanes.T.sum(axis=0, keepdims=True)

        grads = mm(nt_ref[...], dproj_ref[:, cols:], NN) * grad_scale
        gkv_ref[:, :, :pair] = ride_ref[...]
        gkv_ref[:, :, pair:] = grads.reshape(dom_size, width // dom_size, pair).astype(bf16)
        high = dot_ref[...].astype(bf16)
        low = dot_ref[...] - high.astype(f32)
        tail = jnp.concatenate([high.astype(f32), low], axis=0).astype(bf16)
        for k in range(peers):
            pay_refs[k][rows:, :] = tail

    return pl.pallas_call(
        kernel,
        out_shape=(
            jax.ShapeDtypeStruct((dom_size, width // dom_size, 2 * pair), bf16),
            jax.ShapeDtypeStruct((rows, cols), f32),
            jax.ShapeDtypeStruct((blocks, cols), f32),
        )
        + (jax.ShapeDtypeStruct((rows + 2 * blocks, cols), bf16),) * peers,
        in_specs=[smem, hbm] + [vmem] * 7,
        out_specs=(vmem,) * (3 + peers),
        scratch_shapes=[
            pltpu.VMEM((rows, 3 * cols), bf16),
            pltpu.VMEM((sets * blocks, block_len, pair), bf16),
            pltpu.SemaphoreType.DMA((sets * blocks,)),
        ],
        name="finish",
    )(matchings, returned, own, d_query, normed_t, weights, feat, gain, riders)


def input_grad_call(mine, dots, payloads, cotangent, factor, feat_factor):
    rows, cols = mine.shape
    blocks = dots.shape[0]
    block_len = rows // blocks
    peers = len(payloads)

    def kernel(mine_ref, dot_ref, cot_ref, factor_ref, feat_ref, *rest):
        pay_refs = rest[:peers]
        out_ref = rest[peers]
        dots = dot_ref[...]
        for ref in pay_refs:
            tail = ref[rows:, :].astype(f32)
            dots = dots + tail[:blocks] + tail[blocks:]
        for b in range(blocks):
            at = slice(b * block_len, (b + 1) * block_len)
            share = mine_ref[at, :]
            for ref in pay_refs:
                share = share + ref[at, :].astype(f32)
            row_dot = jnp.broadcast_to(dots[b : b + 1, :], (block_len, cols)).T
            out_ref[at, :] = (
                cot_ref[at, :].astype(f32) + factor_ref[at, :] * share - feat_ref[at, :] * row_dot
            ).astype(bf16)

    return pl.pallas_call(
        kernel,
        out_shape=jax.ShapeDtypeStruct((rows, cols), bf16),
        in_specs=[vmem] * (5 + peers),
        out_specs=vmem,
        name="input_grad",
    )(mine, dots, cotangent, factor, feat_factor, *payloads)


def ring(x, axis, step):
    count = lax.axis_size(axis)
    return lax.ppermute(x, axis, [(i, (i + step) % count) for i in range(count)])


def shift_dom(x, step):
    count = lax.axis_size("dom")
    pairs = [(i, i + step) for i in range(count) if 0 <= i + step < count]
    return lax.ppermute(x, "dom", pairs)


def spread(x):
    return lax.all_to_all(x, "dom", split_axis=0, concat_axis=0, tiled=True)


def body(features, norm_gain, qkv_weight, out_weight, edge_bias, band_mask, matchings, cotangent):
    row_count, model_width = features.shape
    local_cols = qkv_weight.shape[2]
    heads_here = edge_bias.shape[0]
    head_size = local_cols // heads_here
    blocks = band_mask.shape[1]
    block_len = row_count // blocks
    dom_size = lax.axis_size("dom")
    dom_index = lax.axis_index("dom")
    head_count = lax.axis_size("head")
    head_index = lax.axis_index("head")
    score_scale = 1.0 / math.sqrt(head_size)
    grad_scale = 1.0 / math.sqrt(dom_size * row_count)
    grad_rows = model_width // dom_size
    pair_cols = 2 * local_cols

    def rolled(x, axis):
        both = jnp.concatenate([x, x], axis=axis)
        return lax.dynamic_slice_in_dim(both, head_index * local_cols, model_width, axis)

    outgoing, keyval, normed, inv_rms = pack_call(
        matchings, features, norm_gain.reshape(1, model_width), qkv_weight, dom_size
    )
    incoming = spread(outgoing)
    before = shift_dom(keyval[-1:], 1)
    after = shift_dom(keyval[:1], -1)
    rimmed = jnp.concatenate([before, keyval, after], axis=0)

    def both_heads(x):
        x = x.reshape(blocks, block_len, local_cols)
        lane = lax.broadcasted_iota(jnp.int32, (1, 1, local_cols), 2) // head_size
        zero = jnp.zeros((), x.dtype)
        return jnp.concatenate([jnp.where(lane == h, x, zero) for h in range(heads_here)], axis=1)

    queries = jnp.dot(normed, qkv_weight[0], preferred_element_type=f32).astype(bf16)
    queries2 = both_heads(queries * jnp.asarray(score_scale, bf16))
    d_attn2 = both_heads(jnp.dot(cotangent, out_weight, preferred_element_type=f32).astype(bf16))
    global_blk = dom_index * blocks + jnp.arange(blocks, dtype=jnp.int32)
    left_ok = (band_mask[0] == 1) & (global_blk > 0)
    right_ok = (band_mask[1] == 1) & (global_blk < dom_size * blocks - 1)
    always = jnp.ones((blocks,), dtype=bool)
    slot_valid = jnp.stack([left_ok, always, right_ok, always, always, always, always])
    bias_blocks = edge_bias.reshape(heads_here, 7, blocks, block_len)
    masked_bias = jnp.where(slot_valid[None, :, :, None], bias_blocks, masked_score)
    masked_bias = masked_bias.transpose(2, 1, 0, 3).reshape(blocks, 7, heads_here * block_len)
    far_grads, near, attended, d_query = attention_call(
        matchings, queries2, d_attn2, masked_bias, rimmed, incoming, score_scale
    )
    returned = spread(far_grads)
    attended = attended.reshape(row_count, local_cols)
    d_query = d_query.reshape(row_count, local_cols)
    rim_left = shift_dom(near[:1].astype(bf16), -1)
    rim_right = shift_dom(near[-1:].astype(bf16), 1)
    own_grads = jnp.concatenate(
        [
            near[1:2] + rim_right.astype(f32),
            near[2:-2],
            near[-2:-1] + rim_left.astype(f32),
        ],
        axis=0,
    )
    grad_out_part = lax.dot_general(
        cotangent, attended, (((0,), (0,)), ((), ())), preferred_element_type=f32
    )
    grad_q_part = lax.dot_general(
        normed, d_query, (((0,), (0,)), ((), ())), preferred_element_type=f32
    )
    riders = jnp.concatenate([grad_out_part * grad_scale, grad_q_part * grad_scale], axis=1)
    riders = riders.astype(bf16).reshape(dom_size, grad_rows, pair_cols)
    partial_out = lax.dot_general(
        attended, rolled(out_weight, 0), (((1,), (1,)), ((), ())), preferred_element_type=f32
    )
    own_feat = lax.dynamic_slice_in_dim(features, head_index * local_cols, local_cols, 1).astype(f32)
    layer_sum = partial_out[:, :local_cols]
    for step in range(1, head_count):
        piece = partial_out[:, step * local_cols : (step + 1) * local_cols].astype(bf16)
        layer_sum = layer_sum + ring(piece, "head", step).astype(f32)
    layer_out = (layer_sum + own_feat).astype(bf16)
    weights = qkv_weight.transpose(1, 0, 2).reshape(model_width, 3 * local_cols)
    own_gain = lax.dynamic_slice_in_dim(norm_gain, head_index * local_cols, local_cols, 0)
    own_cot = lax.dynamic_slice_in_dim(cotangent, head_index * local_cols, local_cols, 1)
    factor = inv_rms * own_gain
    feat_factor = own_feat * (inv_rms * inv_rms * inv_rms / model_width)
    own_grads, layer_out, factor, feat_factor = lax.optimization_barrier(
        (own_grads, layer_out, factor, feat_factor)
    )
    grads, mine, dots, *payloads = finish_call(
        matchings, returned, own_grads, d_query, normed.T, rolled(weights, 0),
        rolled(features, 1), rolled(norm_gain.reshape(1, model_width), 1), riders,
        grad_scale, head_count,
    )
    payloads = [ring(x, "head", step + 1) for step, x in enumerate(payloads)]
    grad_input = input_grad_call(mine, dots, payloads, own_cot, factor, feat_factor)
    grads = jnp.sum(spread(grads).astype(f32), axis=0)
    grad_out, grad_query, grad_key, grad_value = jnp.split(grads, 4, axis=1)
    grad_qkv = jnp.stack([grad_query, grad_key, grad_value])
    return (layer_out, grad_input, grad_qkv, grad_out)


def solution(mesh):
    in_specs = (
        P("dom", None),
        P(),
        P(None, None, "head"),
        P(None, "head"),
        P("head", None, "dom"),
        P(None, "dom"),
        P(None, "dom"),
        P("dom", None),
    )
    out_specs = (P("dom", "head"), P("dom", "head"), P(None, "dom", "head"), P("dom", "head"))
    return jax.shard_map(body, mesh=mesh, in_specs=in_specs, out_specs=out_specs, check_vma=False)
```

```python
import math

import jax
import jax.numpy as jnp
from jax import lax
from jax.experimental import pallas as pl
from jax.experimental.pallas import tpu as pltpu
from jax.sharding import PartitionSpec as P

epsilon_norm = 1e-06
masked_score = -1e30
bf16 = jnp.bfloat16
f32 = jnp.float32
vmem = pl.BlockSpec(memory_space=pltpu.VMEM)
hbm = pl.BlockSpec(memory_space=pl.ANY)
smem = pl.BlockSpec(memory_space=pltpu.SMEM)
NN = (((1,), (0,)), ((), ()))
NT = (((1,), (1,)), ((), ()))
TN = (((0,), (0,)), ((), ()))


def mm(a, b, dims):
    return lax.dot_general(a, b, dims, preferred_element_type=f32)


def pack_call(matchings, features, gain, qkv_weight, dom_size):
    sets, blocks = matchings.shape
    rows, _ = features.shape
    cols = qkv_weight.shape[2]
    block_len = rows // blocks

    def kernel(match_ref, feat_ref, gain_ref, w_ref, slots_ref, kv_ref, sems):
        weight = jnp.concatenate([w_ref[1], w_ref[2]], axis=1)

        def send(b, j):
            slot = slots_ref.at[match_ref[j, b] // blocks]
            return pltpu.make_async_copy(kv_ref.at[b], slot, sems.at[b * sets + j])

        @pl.loop(0, blocks)
        def _(b):
            at = pl.ds(pl.multiple_of(b * block_len, block_len), block_len)
            x = feat_ref[at, :].astype(f32)
            inv = lax.rsqrt(jnp.mean(x * x, axis=1, keepdims=True) + epsilon_norm)
            normed = (x * inv * gain_ref[...]).astype(bf16)
            kv_ref[b] = mm(normed, weight, NN).astype(bf16)
            for j in range(sets):
                send(b, j).start()

        @pl.loop(0, blocks)
        def _(b):
            for j in range(sets):
                send(b, j).wait()

    return pl.pallas_call(
        kernel,
        out_shape=(
            jax.ShapeDtypeStruct((dom_size, block_len, 2 * cols), bf16),
            jax.ShapeDtypeStruct((blocks, block_len, 2 * cols), bf16),
        ),
        in_specs=[smem, vmem, vmem, vmem],
        out_specs=(hbm, vmem),
        scratch_shapes=[pltpu.SemaphoreType.DMA((sets * blocks,))],
        name="pack_slots",
    )(matchings, features, gain, qkv_weight)


def near_stats_call(queries2, d_attn2, bias, rimmed):
    blocks, wide, cols = queries2.shape

    def kernel(q_ref, do_ref, bias_ref, rim_ref, peak_ref, total_ref, pull_ref):
        @pl.loop(0, blocks)
        def _(b):
            q2 = q_ref[b]
            do2 = do_ref[b]
            kv = [rim_ref[b + s] for s in range(3)]
            score = [mm(kv[s][:, :cols], q2, NT) + bias_ref[b, pl.ds(s, 1), :] for s in range(3)]
            peak = score[0].max(axis=0, keepdims=True)
            for x in score[1:]:
                peak = jnp.maximum(peak, x.max(axis=0, keepdims=True))
            weight = [jnp.exp(x - peak) for x in score]
            peak_ref[b] = peak
            total_ref[b] = sum(x.sum(axis=0, keepdims=True) for x in weight)
            pull_ref[b] = sum(
                (weight[s] * mm(kv[s][:, cols:], do2, NT)).sum(axis=0, keepdims=True)
                for s in range(3)
            )

    return pl.pallas_call(
        kernel,
        out_shape=(jax.ShapeDtypeStruct((blocks, 1, wide), f32),) * 3,
        in_specs=[vmem] * 4,
        out_specs=(vmem,) * 3,
        name="near_stats",
    )(queries2, d_attn2, bias, rimmed)


def far_call(matchings, queries2, d_attn2, bias, stats, incoming):
    sets, blocks = matchings.shape
    dom_size, block_len, pair = incoming.shape
    cols = pair // 2

    def kernel(
        match_ref, q_ref, do_ref, bias_ref, peak_ref, total_ref, pull_ref, in_ref,
        out_ref, far_ref, grad_ref, in_sems, out_sems,
    ):
        def fetch(b, j):
            slot = in_ref.at[match_ref[j, b] // blocks]
            at = b * sets + j
            return pltpu.make_async_copy(slot, far_ref.at[at], in_sems.at[at])

        def send(b, j):
            slot = out_ref.at[match_ref[j, b] // blocks]
            at = b * sets + j
            return pltpu.make_async_copy(grad_ref.at[at], slot, out_sems.at[at])

        @pl.loop(0, blocks)
        def _(b):
            for j in range(sets):
                fetch(b, j).start()

        @pl.loop(0, blocks)
        def _(b):
            for j in range(sets):
                fetch(b, j).wait()
            q2 = q_ref[b]
            do2 = do_ref[b]
            kv = [far_ref[b * sets + j] for j in range(sets)]
            row_bias = [bias_ref[b, pl.ds(3 + j, 1), :] for j in range(sets)]
            score = [mm(kv[j][:, :cols], q2, NT) for j in range(sets)]
            peak = peak_ref[b]
            for j in range(sets):
                peak = jnp.maximum(peak, score[j].max(axis=0, keepdims=True) + row_bias[j])
            weight = [jnp.exp(score[j] + (row_bias[j] - peak)) for j in range(sets)]
            near = jnp.exp(peak_ref[b] - peak)
            total = total_ref[b] * near
            for x in weight:
                total = total + x.sum(axis=0, keepdims=True)
            share = 1.0 / total
            prob = [x * share for x in weight]
            pull = [prob[j] * mm(kv[j][:, cols:], do2, NT) for j in range(sets)]
            delta = pull_ref[b] * (near * share)
            for x in pull:
                delta = delta + x.sum(axis=0, keepdims=True)
            for j in range(sets):
                d_score = (pull[j] - prob[j] * delta).astype(bf16)
                grad_ref[b * sets + j, :, :cols] = mm(d_score, q2, NN).astype(bf16)
                grad_ref[b * sets + j, :, cols:] = mm(prob[j].astype(bf16), do2, NN).astype(bf16)
                send(b, j).start()

        @pl.loop(0, blocks)
        def _(b):
            for j in range(sets):
                send(b, j).wait()

    return pl.pallas_call(
        kernel,
        out_shape=jax.ShapeDtypeStruct((dom_size, block_len, pair), bf16),
        in_specs=[smem] + [vmem] * 6 + [hbm],
        out_specs=hbm,
        scratch_shapes=[
            pltpu.VMEM((sets * blocks, block_len, pair), bf16),
            pltpu.VMEM((sets * blocks, block_len, pair), bf16),
            pltpu.SemaphoreType.DMA((sets * blocks,)),
            pltpu.SemaphoreType.DMA((sets * blocks,)),
        ],
        name="far_grads",
    )(matchings, queries2, d_attn2, bias, *stats, incoming)


def attention_call(matchings, queries2, d_attn2, bias, rimmed, incoming, score_scale):
    sets, blocks = matchings.shape
    slots = sets + 3
    _, block_len, pair = incoming.shape
    cols = pair // 2

    def kernel(
        match_ref, q_ref, do_ref, bias_ref, rim_ref, in_ref,
        near_ref, att_ref, dq_ref, far_ref, in_sems,
    ):
        def fetch(b, j):
            slot = in_ref.at[match_ref[j, b] // blocks]
            at = b * sets + j
            return pltpu.make_async_copy(slot, far_ref.at[at], in_sems.at[at])

        @pl.loop(0, blocks)
        def _(b):
            for j in range(sets):
                fetch(b, j).start()

        near_ref[...] = jnp.zeros_like(near_ref)
        half = lax.broadcasted_iota(jnp.int32, (block_len, cols), 1) < cols // 2

        @pl.loop(0, blocks)
        def _(b):
            for j in range(sets):
                fetch(b, j).wait()
            q2 = q_ref[b]
            do2 = do_ref[b]
            kv = [rim_ref[b + s] for s in range(3)] + [far_ref[b * sets + j] for j in range(sets)]
            row_bias = [bias_ref[b, pl.ds(s, 1), :] for s in range(slots)]
            score = [mm(kv[s][:, :cols], q2, NT) for s in range(slots)]
            peak = score[0].max(axis=0, keepdims=True) + row_bias[0]
            for s in range(1, slots):
                peak = jnp.maximum(peak, score[s].max(axis=0, keepdims=True) + row_bias[s])
            weight = [jnp.exp(score[s] + (row_bias[s] - peak)) for s in range(slots)]
            total = weight[0].sum(axis=0, keepdims=True)
            for s in range(1, slots):
                total = total + weight[s].sum(axis=0, keepdims=True)
            share = 1.0 / total
            prob = [x * share for x in weight]
            prob_half = [x.astype(bf16) for x in prob]
            pull = [prob[s] * mm(kv[s][:, cols:], do2, NT) for s in range(slots)]
            delta = pull[0].sum(axis=0, keepdims=True)
            for s in range(1, slots):
                delta = delta + pull[s].sum(axis=0, keepdims=True)
            d_score = [(pull[s] - prob[s] * delta).astype(bf16) for s in range(slots)]
            att = mm(prob_half[0], kv[0][:, cols:], TN)
            d_query = mm(d_score[0], kv[0][:, :cols], TN)
            for s in range(1, slots):
                att = att + mm(prob_half[s], kv[s][:, cols:], TN)
                d_query = d_query + mm(d_score[s], kv[s][:, :cols], TN)
            att_ref[b] = jnp.where(half, att[:block_len], att[block_len:]).astype(bf16)
            dq_ref[b] = (
                jnp.where(half, d_query[:block_len], d_query[block_len:]) * score_scale
            ).astype(bf16)
            for s in range(3):
                near_ref[b + s, :, :cols] += mm(d_score[s], q2, NN)
                near_ref[b + s, :, cols:] += mm(prob_half[s], do2, NN)

    return pl.pallas_call(
        kernel,
        out_shape=(
            jax.ShapeDtypeStruct((blocks + 2, block_len, pair), f32),
            jax.ShapeDtypeStruct((blocks, block_len, cols), bf16),
            jax.ShapeDtypeStruct((blocks, block_len, cols), bf16),
        ),
        in_specs=[smem, vmem, vmem, vmem, vmem, hbm],
        out_specs=(vmem, vmem, vmem),
        scratch_shapes=[
            pltpu.VMEM((sets * blocks, block_len, pair), bf16),
            pltpu.SemaphoreType.DMA((sets * blocks,)),
        ],
        name="attention",
    )(matchings, queries2, d_attn2, bias, rimmed, incoming)


def finish_call(
    matchings, returned, own, d_query, normed_t, weights, feat, gain, grad_scale, heads
):
    sets, blocks = matchings.shape
    dom_size, block_len, pair = returned.shape
    cols = pair // 2
    rows = blocks * block_len
    width = normed_t.shape[0]
    peers = heads - 1

    def kernel(
        match_ref, back_ref, own_ref, dq_ref, nt_ref, w_ref, feat_ref, gain_ref,
        gkv_ref, mine_ref, dot_ref, *rest,
    ):
        pay_refs = rest[:peers]
        dproj_ref, buf_ref, sems = rest[peers:]

        def fetch(b, j):
            slot = back_ref.at[match_ref[j, b] // blocks]
            at = b * sets + j
            return pltpu.make_async_copy(slot, buf_ref.at[at], sems.at[at])

        @pl.loop(0, blocks)
        def _(b):
            for j in range(sets):
                fetch(b, j).start()

        @pl.loop(0, blocks)
        def _(b):
            at = pl.ds(pl.multiple_of(b * block_len, block_len), block_len)
            total = own_ref[b]
            for j in range(sets):
                fetch(b, j).wait()
                total = total + buf_ref[b * sets + j].astype(f32)
            d_proj = jnp.concatenate([dq_ref[at, :], total.astype(bf16)], axis=1)
            dproj_ref[at, :] = d_proj
            d_normed = mm(d_proj, w_ref[...], NT)
            mine_ref[at, :] = d_normed[:, :cols]
            for k in range(peers):
                pay_refs[k][at, :] = d_normed[:, (k + 1) * cols : (k + 2) * cols].astype(bf16)
            moved = d_normed * (feat_ref[at, :].astype(f32) * gain_ref[...])
            lanes = moved[:, :cols]
            for k in range(1, heads):
                lanes = lanes + moved[:, k * cols : (k + 1) * cols]
            dot_ref[pl.ds(b, 1), :] = lanes.T.sum(axis=0, keepdims=True)

        grads = mm(nt_ref[...], dproj_ref[:, cols:], NN) * grad_scale
        gkv_ref[...] = grads.reshape(dom_size, width // dom_size, pair).astype(bf16)
        high = dot_ref[...].astype(bf16)
        low = dot_ref[...] - high.astype(f32)
        tail = jnp.concatenate([high.astype(f32), low], axis=0).astype(bf16)
        for k in range(peers):
            pay_refs[k][rows:, :] = tail

    return pl.pallas_call(
        kernel,
        out_shape=(
            jax.ShapeDtypeStruct((dom_size, width // dom_size, pair), bf16),
            jax.ShapeDtypeStruct((rows, cols), f32),
            jax.ShapeDtypeStruct((blocks, cols), f32),
        )
        + (jax.ShapeDtypeStruct((rows + 2 * blocks, cols), bf16),) * peers,
        in_specs=[smem, hbm] + [vmem] * 6,
        out_specs=(vmem,) * (3 + peers),
        scratch_shapes=[
            pltpu.VMEM((rows, 3 * cols), bf16),
            pltpu.VMEM((sets * blocks, block_len, pair), bf16),
            pltpu.SemaphoreType.DMA((sets * blocks,)),
        ],
        name="finish",
    )(matchings, returned, own, d_query, normed_t, weights, feat, gain)


def input_grad_call(mine, dots, payloads, cotangent, factor, feat_factor):
    rows, cols = mine.shape
    blocks = dots.shape[0]
    block_len = rows // blocks
    peers = len(payloads)

    def kernel(mine_ref, dot_ref, cot_ref, factor_ref, feat_ref, *rest):
        pay_refs = rest[:peers]
        out_ref = rest[peers]
        dots = dot_ref[...]
        for ref in pay_refs:
            tail = ref[rows:, :].astype(f32)
            dots = dots + tail[:blocks] + tail[blocks:]
        for b in range(blocks):
            at = slice(b * block_len, (b + 1) * block_len)
            share = mine_ref[at, :]
            for ref in pay_refs:
                share = share + ref[at, :].astype(f32)
            row_dot = jnp.broadcast_to(dots[b : b + 1, :], (block_len, cols)).T
            out_ref[at, :] = (
                cot_ref[at, :].astype(f32) + factor_ref[at, :] * share - feat_ref[at, :] * row_dot
            ).astype(bf16)

    return pl.pallas_call(
        kernel,
        out_shape=jax.ShapeDtypeStruct((rows, cols), bf16),
        in_specs=[vmem] * (5 + peers),
        out_specs=vmem,
        name="input_grad",
    )(mine, dots, cotangent, factor, feat_factor, *payloads)


def ring(x, axis, step):
    count = lax.axis_size(axis)
    return lax.ppermute(x, axis, [(i, (i + step) % count) for i in range(count)])


def shift_dom(x, step):
    count = lax.axis_size("dom")
    pairs = [(i, i + step) for i in range(count) if 0 <= i + step < count]
    return lax.ppermute(x, "dom", pairs)


def spread(x):
    return lax.all_to_all(x, "dom", split_axis=0, concat_axis=0, tiled=True)


def halving_sum(part):
    count = part.shape[0]
    bits = count.bit_length() - 1
    here = lax.axis_index("dom")
    part = part.reshape((2,) * bits + part.shape[1:])
    order = list(range(bits - 1, -1, -1))
    for bit in [0] + list(range(bits - 1, 0, -1)):
        axis = order.index(bit)
        mine = (here >> bit) & 1
        away = lax.dynamic_index_in_dim(part, 1 - mine, axis, keepdims=False)
        stay = lax.dynamic_index_in_dim(part, mine, axis, keepdims=False)
        part = stay + lax.ppermute(away, "dom", [(i, i ^ (1 << bit)) for i in range(count)])
        order.pop(axis)
    return part


def body(features, norm_gain, qkv_weight, out_weight, edge_bias, band_mask, matchings, cotangent):
    row_count, model_width = features.shape
    local_cols = qkv_weight.shape[2]
    heads_here = edge_bias.shape[0]
    head_size = local_cols // heads_here
    blocks = band_mask.shape[1]
    block_len = row_count // blocks
    dom_size = lax.axis_size("dom")
    dom_index = lax.axis_index("dom")
    head_count = lax.axis_size("head")
    head_index = lax.axis_index("head")
    score_scale = 1.0 / math.sqrt(head_size)
    grad_scale = 1.0 / math.sqrt(dom_size * row_count)
    grad_rows = model_width // dom_size
    pair_cols = 2 * local_cols

    def rolled(x, axis):
        both = jnp.concatenate([x, x], axis=axis)
        return lax.dynamic_slice_in_dim(both, head_index * local_cols, model_width, axis)

    outgoing, keyval = pack_call(
        matchings, features, norm_gain.reshape(1, model_width), qkv_weight, dom_size
    )
    incoming = spread(outgoing)
    feat_f32 = features.astype(f32)
    inv_rms = lax.rsqrt(jnp.mean(feat_f32 * feat_f32, axis=1, keepdims=True) + epsilon_norm)
    normed = (feat_f32 * inv_rms * norm_gain).astype(bf16)
    before = shift_dom(keyval[-1:], 1)
    after = shift_dom(keyval[:1], -1)
    rimmed = jnp.concatenate([before, keyval, after], axis=0)

    def both_heads(x):
        x = x.reshape(blocks, block_len, local_cols)
        lane = lax.broadcasted_iota(jnp.int32, (1, 1, local_cols), 2) // head_size
        zero = jnp.zeros((), x.dtype)
        return jnp.concatenate([jnp.where(lane == h, x, zero) for h in range(heads_here)], axis=1)

    queries = jnp.dot(normed, qkv_weight[0], preferred_element_type=f32).astype(bf16)
    queries2 = both_heads(queries * jnp.asarray(score_scale, bf16))
    d_attn2 = both_heads(jnp.dot(cotangent, out_weight, preferred_element_type=f32).astype(bf16))
    global_blk = dom_index * blocks + jnp.arange(blocks, dtype=jnp.int32)
    left_ok = (band_mask[0] == 1) & (global_blk > 0)
    right_ok = (band_mask[1] == 1) & (global_blk < dom_size * blocks - 1)
    always = jnp.ones((blocks,), dtype=bool)
    slot_valid = jnp.stack([left_ok, always, right_ok, always, always, always, always])
    bias_blocks = edge_bias.reshape(heads_here, 7, blocks, block_len)
    masked_bias = jnp.where(slot_valid[None, :, :, None], bias_blocks, masked_score)
    masked_bias = masked_bias.transpose(2, 1, 0, 3).reshape(blocks, 7, heads_here * block_len)
    stats = near_stats_call(queries2, d_attn2, masked_bias, rimmed)
    far_grads = far_call(matchings, queries2, d_attn2, masked_bias, stats, incoming)
    returned = spread(far_grads)
    near, attended, d_query = attention_call(
        matchings, queries2, d_attn2, masked_bias, rimmed, incoming, score_scale
    )
    attended = attended.reshape(row_count, local_cols)
    d_query = d_query.reshape(row_count, local_cols)
    rim_left = shift_dom(near[:1].astype(bf16), -1)
    rim_right = shift_dom(near[-1:].astype(bf16), 1)
    own_grads = jnp.concatenate(
        [
            near[1:2] + rim_right.astype(f32),
            near[2:-2],
            near[-2:-1] + rim_left.astype(f32),
        ],
        axis=0,
    )
    grad_out_part = lax.dot_general(
        cotangent, attended, (((0,), (0,)), ((), ())), preferred_element_type=f32
    )
    grad_q_part = lax.dot_general(
        normed, d_query, (((0,), (0,)), ((), ())), preferred_element_type=f32
    )
    riders = jnp.concatenate([grad_out_part * grad_scale, grad_q_part * grad_scale], axis=1)
    grads_oq = halving_sum(riders.reshape(dom_size, grad_rows, pair_cols))
    partial_out = lax.dot_general(
        attended, rolled(out_weight, 0), (((1,), (1,)), ((), ())), preferred_element_type=f32
    )
    own_feat = lax.dynamic_slice_in_dim(features, head_index * local_cols, local_cols, 1).astype(f32)
    layer_sum = partial_out[:, :local_cols]
    for step in range(1, head_count):
        piece = partial_out[:, step * local_cols : (step + 1) * local_cols].astype(bf16)
        layer_sum = layer_sum + ring(piece, "head", step).astype(f32)
    layer_out = (layer_sum + own_feat).astype(bf16)
    weights = qkv_weight.transpose(1, 0, 2).reshape(model_width, 3 * local_cols)
    own_gain = lax.dynamic_slice_in_dim(norm_gain, head_index * local_cols, local_cols, 0)
    own_cot = lax.dynamic_slice_in_dim(cotangent, head_index * local_cols, local_cols, 1)
    factor = inv_rms * own_gain
    feat_factor = own_feat * (inv_rms * inv_rms * inv_rms / model_width)
    own_grads, layer_out, factor, feat_factor, grads_oq = lax.optimization_barrier(
        (own_grads, layer_out, factor, feat_factor, grads_oq)
    )
    grads, mine, dots, *payloads = finish_call(
        matchings, returned, own_grads, d_query, normed.T, rolled(weights, 0),
        rolled(features, 1), rolled(norm_gain.reshape(1, model_width), 1),
        grad_scale, head_count,
    )
    moved = []
    for step, x in enumerate(payloads):
        moved.append(ring(x, "head", step + 1))
    payloads = moved
    grads = spread(grads)
    grad_input = input_grad_call(mine, dots, payloads, own_cot, factor, feat_factor)
    grads = jnp.sum(grads.astype(f32), axis=0)
    grad_out, grad_query = jnp.split(grads_oq, 2, axis=1)
    grad_key, grad_value = jnp.split(grads, 2, axis=1)
    grad_qkv = jnp.stack([grad_query, grad_key, grad_value])
    return (layer_out, grad_input, grad_qkv, grad_out)


def solution(mesh):
    in_specs = (
        P("dom", None),
        P(),
        P(None, None, "head"),
        P(None, "head"),
        P("head", None, "dom"),
        P(None, "dom"),
        P(None, "dom"),
        P("dom", None),
    )
    out_specs = (P("dom", "head"), P("dom", "head"), P(None, "dom", "head"), P("dom", "head"))
    return jax.shard_map(
        body, mesh=mesh, in_specs=in_specs, out_specs=out_specs, check_vma=False
    )
```
